32 devices in a mesh: ctx: 4 (over y, x), head: 4 (over z), pool: 2 (over core).
Axes of the slice: x: 2, y: 2, z: 4, core: 2. Of those that a mesh axis runs over, the one named last changes fastest.
Arguments:
- queries: bfloat16 [256, 64, 128], P(None, 'head'), may hold values from -200 to 200
- prefix_keys: bfloat16 [2048, 8, 128], P(('ctx', 'pool'), 'head'), may hold values from -6 to 6
- prefix_values: bfloat16 [2048, 8, 128], P(('ctx', 'pool'), 'head'), may hold values from -6 to 6
- new_states: bfloat16 [384, 8192], P(None, ('ctx', 'pool')), may hold values from -7 to 7
- key_weight: bfloat16 [8192, 1024], P(('ctx', 'pool'), 'head'), may hold values from -0.0625 to 0.0625
- value_weight: bfloat16 [8192, 1024], P(('ctx', 'pool'), 'head'), may hold values from -0.0625 to 0.0625
- suffix_keys: bfloat16 [8, 256, 8, 128], P(('ctx', 'pool'), None, 'head'), may hold values from -8 to 8
- suffix_values: bfloat16 [8, 256, 8, 128], P(('ctx', 'pool'), None, 'head'), may hold values from -6 to 6
- suffix_lengths: int32 [8], P(('ctx', 'pool')), may hold values from 1 to 256
- assignment: int32 [256], replicated, may hold values from 0 to 7
- out_weight: bfloat16 [8192, 8192], P('head', ('ctx', 'pool')), may hold values from -0.25 to 0.25
Outputs:
- projected: bfloat16 [256, 8192], P('head', ('ctx', 'pool'))
- new_keys: bfloat16 [384, 8, 128], P(('ctx', 'pool'), 'head')
- new_values: bfloat16 [384, 8, 128], P(('ctx', 'pool'), 'head')
The draws below stay inside these ranges and needn't reach their ends.
All inputs are finite; a program needn't handle non-finite values.
Results may differ from the reference program's by a relative error of at most 0.0102.
Values may be sent and summed in bfloat16 or wider, within the bound.
No kernel may reach another device: no remote copies, remote signals or barrier semaphores. Data moves between devices by JAX's collectives and lax.ppermute only.
A program may use at most 64 MiB of HBM per device.

```python
import math
import jax
import jax.numpy as jnp
from jax import lax

D = 8192
HQ = 64
KVH = 8
HD = 128
PART = 256
SLEN = 256
PREFIX = 2048
NEW = 384
SUF = 8


def shared_draw(key):
    base_key = jax.random.fold_in(key, 7)
    key_one, key_two = jax.random.split(base_key, 2)
    cached = jnp.clip(jax.random.normal(key_one, (PREFIX, KVH, HD), jnp.float32), -6.0, 6.0)
    asked = jnp.clip(2.5 * jax.random.normal(key_two, (PART, HQ, HD), jnp.float32), -15.0, 15.0)
    return (asked, cached)


def draw_queries(key, part):
    return shared_draw(key)[0].astype(jnp.bfloat16)


def draw_prefix_keys(key, part):
    return shared_draw(key)[1].astype(jnp.bfloat16)


def plant(entries, rng, least, high):
    extent = entries.shape
    index_at = [jax.random.randint(jax.random.fold_in(rng, axis), (), 0, extent[axis]) for axis in range(len(extent))]
    entries = entries.at[tuple(index_at)].set(least)
    longest = extent.index(max(extent))
    index_at[longest] = (index_at[longest] + 1) % extent[longest]
    return entries.at[tuple(index_at)].set(high)


def levels(key, extent, shards, low, top_value):
    factor_of, own = 1.0, jax.random.fold_in(key, 6)
    for dim, shards_of in shards:
        steps = jnp.exp(jax.random.uniform(jax.random.fold_in(own, dim), (shards_of,), jnp.float32, low / len(shards), top_value / len(shards)))
        factor_of = factor_of * jnp.repeat(steps, extent[dim] // shards_of).reshape([-1 if axis == dim else 1 for axis in range(len(extent))])
    return factor_of


def normal_values(key, extent, scale, reach, cuts=(), kind=jnp.bfloat16):
    values = jax.random.normal(key, extent, jnp.float32) * scale
    if len(cuts) > 0:
        values = levels(key, extent, cuts, -0.22, 0.18) * values
    return jnp.clip(values, min=-reach, max=reach).astype(kind)


def setup_inputs(seed: int = 0) -> dict:
    keys = jax.random.split(jax.random.key(seed), 12)
    queries = draw_queries(jax.random.fold_in(keys[11], 71), 0)
    prefix_keys = draw_prefix_keys(jax.random.fold_in(keys[11], 71), 0)
    prefix_values = normal_values(keys[2], (PREFIX, KVH, HD), 1.0, 6.0, ((0, 8), (1, 4)))
    new_states = normal_values(keys[3], (NEW, D), 1.2, 7.0, ((1, 8),))
    key_weight = normal_values(keys[4], (D, KVH * HD), D ** -0.5, 0.0625, ((0, 8), (1, 4)))
    value_weight = normal_values(keys[5], (D, KVH * HD), D ** -0.5, 0.0625, ((0, 8), (1, 4)))
    suffix_keys = normal_values(keys[6], (SUF, SLEN, KVH, HD), 1.4, 8.0, ((0, 8), (2, 4)))
    suffix_values = normal_values(keys[7], (SUF, SLEN, KVH, HD), 1.0, 6.0, ((0, 8), (2, 4)))
    suffix_lengths = plant(jax.random.randint(keys[8], (SUF,), 1, SLEN + 1), jax.random.fold_in(keys[8], 1), 1, SLEN).astype(jnp.int32)
    assignment = plant(jax.random.randint(keys[9], (PART,), 0, SUF), jax.random.fold_in(keys[9], 1), 0, SUF - 1).astype(jnp.int32)
    out_weight = normal_values(keys[10], (HQ * HD, D), (D // 16) ** -0.5, 0.25, ((0, 4), (1, 8)))
    return dict(queries=queries, prefix_keys=prefix_keys, prefix_values=prefix_values, new_states=new_states, key_weight=key_weight, value_weight=value_weight, suffix_keys=suffix_keys, suffix_values=suffix_values, suffix_lengths=suffix_lengths, assignment=assignment, out_weight=out_weight)


def rotate(values, positions):
    half_dim = values.shape[-1] // 2
    frequency = jnp.exp(jnp.arange(half_dim, dtype=jnp.float32) * (-2.0 * math.log(500000.0) / values.shape[-1]))
    angles = positions.astype(jnp.float32)[:, None] * frequency[None, :]
    cosine = jnp.cos(angles)[:, None, :]
    sine_part = jnp.sin(angles)[:, None, :]
    front = values[..., :half_dim]
    second = values[..., half_dim:]
    return jnp.concatenate([front * cosine - second * sine_part, second * cosine + front * sine_part], -1)


def attend_group(group_queries, group_keys, group_values, chosen_keys, chosen_values, usable):
    group_size = group_queries.shape[1]
    key_count = group_keys.shape[0]
    block_rows = math.gcd(PART, 128)
    block_count = PART // block_rows
    inv_scale = HD ** -0.5

    def one_block(inputs):
        block_q, block_k, block_v, block_use = inputs
        query_rows = block_q.reshape(block_rows * group_size, HD)
        main_scores = jnp.dot(query_rows, group_keys.T, preferred_element_type=jnp.float32) * inv_scale
        main_scores = main_scores.reshape(block_rows, group_size, key_count)
        side_scores = jnp.einsum("pgd,psd->pgs", block_q.astype(jnp.float32), block_k.astype(jnp.float32)) * inv_scale
        side_scores = jnp.where(block_use[:, None, :], side_scores, -jnp.inf)
        maxima = jnp.maximum(jnp.max(main_scores, -1), jnp.max(side_scores, -1))
        main_exp = jnp.exp(main_scores - maxima[..., None])
        side_exp = jnp.exp(side_scores - maxima[..., None])
        totals = jnp.sum(main_exp, -1) + jnp.sum(side_exp, -1)
        main_part = jnp.dot(main_exp.astype(jnp.bfloat16).reshape(block_rows * group_size, key_count), group_values, preferred_element_type=jnp.float32)
        side_part = jnp.einsum("pgs,psd->pgd", side_exp.astype(jnp.bfloat16).astype(jnp.float32), block_v.astype(jnp.float32))
        weighted = main_part.reshape(block_rows, group_size, HD) + side_part
        return (weighted / totals[..., None]).astype(jnp.bfloat16)

    inputs = (group_queries.reshape(block_count, block_rows, group_size, HD),
              chosen_keys.reshape(block_count, block_rows, SLEN, HD),
              chosen_values.reshape(block_count, block_rows, SLEN, HD),
              usable.reshape(block_count, block_rows, SLEN))
    return lax.map(one_block, inputs).reshape(PART, group_size, HD)


def reference(queries, prefix_keys, prefix_values, new_states, key_weight, value_weight, suffix_keys, suffix_values, suffix_lengths, assignment, out_weight):
    group_size = HQ // KVH
    raw_keys = jnp.dot(new_states, key_weight, preferred_element_type=jnp.float32).reshape(NEW, KVH, HD)
    positions = PREFIX + jnp.arange(NEW, dtype=jnp.int32)
    new_keys = rotate(raw_keys, positions).astype(jnp.bfloat16)
    new_values = jnp.dot(new_states, value_weight, preferred_element_type=jnp.float32).reshape(NEW, KVH, HD).astype(jnp.bfloat16)
    keys_all = jnp.concatenate([prefix_keys, new_keys], 0).transpose(1, 0, 2)
    values_all = jnp.concatenate([prefix_values, new_values], 0).transpose(1, 0, 2)
    query_groups = queries.reshape(PART, KVH, group_size, HD).transpose(1, 0, 2, 3)
    usable = jnp.arange(SLEN, dtype=jnp.int32)[None, :] < suffix_lengths[assignment][:, None]

    def per_group(inputs):
        group_queries, group_keys, group_values, side_keys, side_values = inputs
        return attend_group(group_queries, group_keys, group_values, side_keys[assignment], side_values[assignment], usable)

    attention = lax.map(per_group, (query_groups, keys_all, values_all, suffix_keys.transpose(2, 0, 1, 3), suffix_values.transpose(2, 0, 1, 3)))
    attention = attention.transpose(1, 0, 2, 3).reshape(PART, HQ * HD)
    projected = jnp.dot(attention, out_weight, preferred_element_type=jnp.float32).astype(jnp.bfloat16)
    return (projected, new_keys, new_values)
```

```python
import functools
import math

import jax
import jax.numpy as jnp
from jax import lax
from jax.experimental import pallas as pl
from jax.experimental.pallas import tpu as pltpu
from jax.sharding import PartitionSpec as P


F32 = jnp.float32
BF16 = jnp.bfloat16
LANES = 128
MASKED = -1e30


def mate(i, s, n):
    return i ^ s if n & (n - 1) == 0 else (i + s) % n


def back(i, s, n):
    return i ^ s if n & (n - 1) == 0 else lax.rem(i - s + n, n)


def forth(i, s, n):
    return i ^ s if n & (n - 1) == 0 else lax.rem(i + s, n)


def send(x, axis, s, n):
    return lax.ppermute(x, axis, [(i, mate(i, s, n)) for i in range(n)])


def split2(x):
    high = x.astype(BF16)
    return high, (x - high.astype(F32)).astype(BF16)


def vmem():
    return pl.BlockSpec(memory_space=pltpu.VMEM)


def smem():
    return pl.BlockSpec(memory_space=pltpu.SMEM)


def eye_block(rows):
    r = lax.broadcasted_iota(jnp.int32, (rows, LANES), 0)
    c = lax.broadcasted_iota(jnp.int32, (rows, LANES), 1)
    return r == c


def project_kernel(ctx, rows, width, pos_ref, x_ref, k_ref, v_ref, keep_ref, send_ref, acc_k, acc_v):
    step = pl.program_id(0)

    @pl.when(step == 0)
    def _():
        acc_k[...] = jnp.zeros_like(acc_k)
        acc_v[...] = jnp.zeros_like(acc_v)

    acc_k[...] += jnp.dot(x_ref[...], k_ref[...], preferred_element_type=F32)
    acc_v[...] += jnp.dot(x_ref[...], v_ref[...], preferred_element_type=F32)

    @pl.when(step == pl.num_programs(0) - 1)
    def _():
        p = pos_ref[1]
        for c in range(ctx):
            mine = pl.ds((2 * c + p) * rows, rows)
            other = pl.ds((2 * c + 1 - p) * rows, rows)
            keep_ref[c, :, :width] = acc_k[mine, :]
            keep_ref[c, :, width:] = acc_v[mine, :]
            high, low = split2(acc_k[other, :])
            send_ref[c, :, :width] = high
            send_ref[c, :, width : 2 * width] = low
            send_ref[c, :, 2 * width :] = acc_v[other, :].astype(BF16)


def project(pos, states, key_weight, value_weight, ctx):
    tokens, feats = states.shape
    width = key_weight.shape[1]
    rows = tokens // (2 * ctx)
    steps = 4 if feats % 512 == 0 else 1
    part = feats // steps
    return pl.pallas_call(
        functools.partial(project_kernel, ctx, rows, width),
        grid=(steps,),
        in_specs=[
            smem(),
            pl.BlockSpec((tokens, part), lambda i: (0, i)),
            pl.BlockSpec((part, width), lambda i: (i, 0)),
            pl.BlockSpec((part, width), lambda i: (i, 0)),
        ],
        out_specs=[
            pl.BlockSpec((ctx, rows, 2 * width), lambda i: (0, 0, 0)),
            pl.BlockSpec((ctx, rows, 3 * width), lambda i: (0, 0, 0)),
        ],
        out_shape=[
            jax.ShapeDtypeStruct((ctx, rows, 2 * width), F32),
            jax.ShapeDtypeStruct((ctx, rows, 3 * width), BF16),
        ],
        scratch_shapes=[pltpu.VMEM((tokens, width), F32), pltpu.VMEM((tokens, width), F32)],
        name="project_new",
    )(pos, states, key_weight, value_weight)


def pair_add_kernel(ctx, width, pos_ref, keep_ref, got_ref, own_ref, *out_refs):
    c = pos_ref[0]
    for s in range(ctx):
        to = forth(c, s, ctx)
        k = keep_ref[to, :, :width] + (
            got_ref[to, :, :width].astype(F32) + got_ref[to, :, width : 2 * width].astype(F32)
        )
        v = keep_ref[to, :, width:] + got_ref[to, :, 2 * width :].astype(F32)
        if s == 0:
            own_ref[:, :width] = k
            own_ref[:, width:] = v
        else:
            high, low = split2(k)
            out_refs[s - 1][:, :width] = high
            out_refs[s - 1][:, width : 2 * width] = low
            out_refs[s - 1][:, 2 * width :] = v.astype(BF16)


def pair_add(pos, keep, got, ctx):
    rows, double = keep.shape[1:]
    width = double // 2
    return pl.pallas_call(
        functools.partial(pair_add_kernel, ctx, width),
        in_specs=[smem(), vmem(), vmem()],
        out_specs=[vmem()] * ctx,
        out_shape=[jax.ShapeDtypeStruct((rows, double), F32)]
        + [jax.ShapeDtypeStruct((rows, 3 * width), BF16)] * (ctx - 1),
        name="pair_add",
    )(pos, keep, got)


def finish_new_kernel(width, cos_ref, sin_ref, own_ref, *refs):
    got, out_ref = refs[:-1], refs[-1]
    for i in range(width // LANES):
        lanes = slice(i * LANES, (i + 1) * LANES)
        k = own_ref[:, lanes]
        v = own_ref[:, width + i * LANES : width + (i + 1) * LANES]
        for g in got:
            k = k + (
                g[:, lanes].astype(F32)
                + g[:, width + i * LANES : width + (i + 1) * LANES].astype(F32)
            )
            v = v + g[:, 2 * width + i * LANES : 2 * width + (i + 1) * LANES].astype(F32)
        turned = k * cos_ref[...] + pltpu.roll(k, LANES // 2, 1) * sin_ref[...]
        out_ref[:, lanes] = turned.astype(BF16)
        out_ref[:, width + i * LANES : width + (i + 1) * LANES] = v.astype(BF16)


def finish_new(cosine, sine, own, got):
    rows, double = own.shape
    return pl.pallas_call(
        functools.partial(finish_new_kernel, double // 2),
        in_specs=[vmem()] * (3 + len(got)),
        out_specs=vmem(),
        out_shape=jax.ShapeDtypeStruct((rows, double), BF16),
        name="finish_new",
    )(cosine, sine, own, *got)


def take_queries(q_ref, start, particles, heads, g, group):
    block = q_ref[pl.ds(start * heads, particles * heads), :]
    if heads == group:
        return block
    wide = block.astype(F32).reshape(particles, heads, LANES)
    part = wide[:, g * group : (g + 1) * group]
    return part.reshape(particles * group, LANES).astype(BF16)


def row_of(column):
    rows = column.shape[0]
    size = min(rows, LANES)
    eye = eye_block(size)
    return [
        jnp.sum(jnp.where(eye, column[b * size : (b + 1) * size], 0.0), axis=0, keepdims=True)
        for b in range(rows // size)
    ]


def column_of(row, size):
    return jnp.sum(jnp.where(eye_block(size), row, 0.0), axis=1, keepdims=True)


def soft(q, keys, values, factor):
    s = lax.dot_general(q, keys, (((1,), (1,)), ((), ())), preferred_element_type=F32)
    m = jnp.max(s, axis=1, keepdims=True) * factor
    w = jnp.exp2(s * factor - m).astype(BF16)
    acc = jnp.dot(w, values, preferred_element_type=F32)
    total = acc[:, LANES:]
    return acc[:, :LANES] / total, m + jnp.log2(total)


def cached_kernel(
    ctx,
    kvs,
    group,
    side,
    factor,
    pos_ref,
    len0_ref,
    len1_ref,
    q_ref,
    hot_ref,
    pk0,
    pv0,
    pk1,
    pv1,
    sk0,
    sv0,
    sk1,
    sv1,
    o_ref,
    l_ref,
    key_s,
    val_s,
    flat,
):
    c, p = pos_ref[0], pos_ref[1]
    heads = kvs * group
    chunk = q_ref.shape[0] // heads // (2 * ctx)
    key_s[...] = jnp.zeros_like(key_s)
    val_s[...] = jnp.ones_like(val_s)
    offset = 0
    for ks, vs in ((pk0, pv0), (pk1, pv1), (sk0, sv0), (sk1, sv1)):
        count = ks.shape[0] // kvs
        for src, dst in ((ks, key_s), (vs, val_s)):
            if kvs > 1:
                flat[: ks.shape[0], :] = src[...].astype(F32)
            for g in range(kvs):
                rows = flat[pl.ds(g, count, stride=kvs), :].astype(BF16) if kvs > 1 else src[...]
                dst[g, offset : offset + count, :LANES] = rows
        offset += count
    offset = (pk0.shape[0] + pk1.shape[0]) // kvs
    length = sk0.shape[0] // kvs // side
    for u, lens in enumerate((len0_ref, len1_ref)):
        shard = 2 * c + (p if u == 0 else 1 - p)
        for a in range(side):
            rows = lax.broadcasted_iota(jnp.int32, (length, LANES), 0)
            lanes = lax.broadcasted_iota(jnp.int32, (length, LANES), 1)
            usable = (lanes == shard * side + a) & (rows < lens[a])
            bias = jnp.where(usable, 0.0, MASKED).astype(BF16)
            for g in range(kvs):
                key_s[g, offset : offset + length, LANES:] = bias
            offset += length

    def one(j, carry):
        start = (2 * j + p) * chunk
        hot = hot_ref[pl.ds(start, chunk), :]
        hot = jnp.broadcast_to(hot[:, None, :], (chunk, group, LANES))
        hot = hot.reshape(chunk * group, LANES).astype(BF16)
        for g in range(kvs):
            q = take_queries(q_ref, start, chunk, heads, g, group)
            o, lse = soft(jnp.concatenate([q, hot], 1), key_s[g], val_s[g], factor)
            o_ref[j, g] = o
            for b, row in enumerate(row_of(lse)):
                l_ref[j, g, b : b + 1, :] = row
        return carry

    lax.fori_loop(0, ctx, one, 0)


def cached(pos, lens, queries, hot, arrays, ctx, kvs, group, side, factor):
    rows = queries.shape[0] // kvs // (2 * ctx)
    blocks = max(1, rows // LANES)
    keys = sum(a.shape[0] for a in arrays[::2]) // kvs
    return pl.pallas_call(
        functools.partial(cached_kernel, ctx, kvs, group, side, factor),
        in_specs=[smem()] * 3 + [vmem()] * 10,
        out_specs=[vmem(), vmem()],
        out_shape=[
            jax.ShapeDtypeStruct((ctx, kvs, rows, LANES), F32),
            jax.ShapeDtypeStruct((ctx, kvs, blocks, LANES), F32),
        ],
        scratch_shapes=[
            pltpu.VMEM((kvs, keys, 2 * LANES), BF16),
            pltpu.VMEM((kvs, keys, 2 * LANES), BF16),
            pltpu.VMEM((max(a.shape[0] for a in arrays), LANES), F32),
        ],
        name="attend_cached",
    )(pos, *lens, queries, hot, *arrays)


def fresh_kernel(ctx, kvs, group, factor, pos_ref, q_ref, n0, n1, o_ref, l_ref, *refs):
    outs, (key_s, val_s, stat) = refs[:ctx], refs[ctx:]
    c, p = pos_ref[0], pos_ref[1]
    heads = kvs * group
    chunk = q_ref.shape[0] // heads // (2 * ctx)
    rows = chunk * group
    size = min(rows, LANES)
    blocks = rows // size
    many = kvs * blocks
    width = kvs * LANES
    val_s[...] = jnp.ones_like(val_s)
    offset = 0
    for src in (n0, n1):
        count = src.shape[0]
        for g in range(kvs):
            key_s[g, offset : offset + count, :] = src[:, g * LANES : (g + 1) * LANES]
            val_s[g, offset : offset + count, :LANES] = src[
                :, width + g * LANES : width + (g + 1) * LANES
            ]
        offset += count
    stat[...] = jnp.zeros_like(stat)
    for s in range(ctx):
        j = forth(c, s, ctx)
        start = (2 * j + p) * chunk
        for g in range(kvs):
            q = take_queries(q_ref, start, chunk, heads, g, group)
            o_new, l_new = soft(q, key_s[g], val_s[g], factor)
            former = l_ref[j, g]
            l_old = jnp.concatenate(
                [column_of(former[b : b + 1, :], size) for b in range(blocks)], 0
            )
            top = jnp.maximum(l_old, l_new)
            w_old = jnp.exp2(l_old - top)
            w_new = jnp.exp2(l_new - top)
            total = w_old + w_new
            o = (o_ref[j, g] * w_old + o_new * w_new) / total
            outs[s][g * rows : (g + 1) * rows, :] = o.astype(BF16)
            for b, row in enumerate(row_of(top + jnp.log2(total))):
                stat[g * blocks + b : g * blocks + b + 1, :] = row
        lse = stat[:many, :]
        high = lse.astype(BF16).astype(F32)
        middle = (lse - high).astype(BF16).astype(F32)
        low = lse - high - middle
        extra = outs[s].shape[0] - kvs * rows
        parts = [high, middle, low]
        if extra > 3 * many:
            parts.append(jnp.zeros((extra - 3 * many, LANES), F32))
        outs[s][kvs * rows :, :] = jnp.concatenate(parts, 0).astype(BF16)


def extra_rows(kvs, rows):
    return -(-3 * kvs * max(1, rows // LANES) // 16) * 16


def fresh(pos, queries, own, other, o, lse, ctx, kvs, group, factor):
    rows = o.shape[2]
    blocks = lse.shape[2]
    tokens = own.shape[0] + other.shape[0]
    total = kvs * rows + extra_rows(kvs, rows)
    return pl.pallas_call(
        functools.partial(fresh_kernel, ctx, kvs, group, factor),
        in_specs=[smem()] + [vmem()] * 5,
        out_specs=[vmem()] * ctx,
        out_shape=[jax.ShapeDtypeStruct((total, LANES), BF16)] * ctx,
        scratch_shapes=[
            pltpu.VMEM((kvs, tokens, LANES), BF16),
            pltpu.VMEM((kvs, tokens, 2 * LANES), BF16),
            pltpu.VMEM((max(8, -(-kvs * blocks // 8) * 8), LANES), F32),
        ],
        name="attend_new",
    )(pos, queries, own, other, o, lse)


def merge_kernel(kvs, group, rows, *refs):
    parts, out_ref, wide = refs[:-2], refs[-2], refs[-1]
    size = min(rows, LANES)
    many = kvs * (rows // size)
    top = None
    stats = []
    for ref in parts:
        stat = ref[kvs * rows :, :].astype(F32)
        lse = stat[:many] + (stat[many : 2 * many] + stat[2 * many : 3 * many])
        stats.append(lse)
        top = lse if top is None else jnp.maximum(top, lse)
    weights = [jnp.exp2(lse - top) for lse in stats]
    total = functools.reduce(lambda a, b: a + b, weights)
    weights = [w / total for w in weights]
    for b in range(many):
        acc = None
        for ref, w in zip(parts, weights):
            column = column_of(w[b : b + 1, :], size)
            term = ref[b * size : (b + 1) * size, :].astype(F32) * column
            acc = term if acc is None else acc + term
        wide[b * size : (b + 1) * size, :] = acc
    chunk = rows // group
    for g in range(kvs):
        for h in range(group):
            at = (g * group + h) * LANES
            out_ref[:, at : at + LANES] = wide[
                pl.ds(g * rows + h, chunk, stride=group), :
            ].astype(BF16)


def merge(parts, kvs, group, rows):
    return pl.pallas_call(
        functools.partial(merge_kernel, kvs, group, rows),
        in_specs=[vmem()] * len(parts),
        out_specs=vmem(),
        out_shape=jax.ShapeDtypeStruct((rows // group, kvs * group * LANES), BF16),
        scratch_shapes=[pltpu.VMEM((kvs * rows, LANES), F32)],
        name="merge_parts",
    )(*parts)


def out_kernel(ctx, peers, pos_ref, w_ref, *refs):
    pieces, outs, (lhs, result) = refs[:ctx], refs[ctx : ctx + peers], refs[ctx + peers :]
    c, h = pos_ref[0], pos_ref[2]
    chunk = pieces[0].shape[0]
    share = ctx // peers * chunk

    @pl.when(pl.program_id(0) == 0)
    def _():
        for s in range(ctx):
            lhs[pl.ds(back(c, s, ctx) * chunk, chunk), :] = pieces[s][...]

    result[...] = jnp.dot(lhs[...], w_ref[...], preferred_element_type=F32)
    for r in range(peers):
        outs[r][...] = result[pl.ds(forth(h, r, peers) * share, share), :].astype(outs[r].dtype)


def out_project(pos, weight, pieces, ctx, peers):
    chunk, depth = pieces[0].shape
    columns = weight.shape[1]
    block = math.gcd(columns, 256)
    share = ctx // peers * chunk
    return pl.pallas_call(
        functools.partial(out_kernel, ctx, peers),
        grid=(columns // block,),
        in_specs=[smem(), pl.BlockSpec((depth, block), lambda i: (0, i))] + [vmem()] * ctx,
        out_specs=[pl.BlockSpec((share, block), lambda i: (0, i))] * peers,
        out_shape=[
            jax.ShapeDtypeStruct((share, columns), F32 if r == 0 else BF16) for r in range(peers)
        ],
        scratch_shapes=[
            pltpu.VMEM((ctx * chunk, depth), BF16),
            pltpu.VMEM((ctx * chunk, block), F32),
        ],
        name="out_project",
    )(pos, weight, *pieces)


def body(
    queries,
    prefix_keys,
    prefix_values,
    new_states,
    key_weight,
    value_weight,
    suffix_keys,
    suffix_values,
    suffix_lengths,
    assignment,
    out_weight,
):
    ctx, peers = lax.axis_size("ctx"), lax.axis_size("head")
    c, p, h = lax.axis_index("ctx"), lax.axis_index("pool"), lax.axis_index("head")
    pos = jnp.stack([c, p, h]).astype(jnp.int32)
    shards = 2 * ctx
    particles, heads, head_dim = queries.shape
    kvs = prefix_keys.shape[1]
    group = heads // kvs
    side = suffix_keys.shape[0]
    width = kvs * head_dim
    factor = head_dim ** (-0.5) / math.log(2.0)

    flat = [
        a.reshape(-1, head_dim) for a in (prefix_keys, prefix_values, suffix_keys, suffix_values)
    ]
    swapped = [send(a, "pool", 1, 2) for a in flat]
    lens = (suffix_lengths, send(suffix_lengths, "pool", 1, 2))
    arrays = (
        flat[0], flat[1], swapped[0], swapped[1], flat[2], flat[3], swapped[2], swapped[3],
    )

    keep, give = project(pos, new_states, key_weight, value_weight, ctx)
    new_dev = keep.shape[1]
    own, *gives = pair_add(pos, keep, send(give, "pool", 1, 2), ctx)
    got = [send(x, "ctx", s + 1, ctx) for s, x in enumerate(gives)]

    hot = (assignment[:, None] == jnp.arange(LANES, dtype=jnp.int32)[None, :]).astype(F32)
    q_rows = queries.reshape(particles * heads, head_dim)
    o, lse = cached(pos, lens, q_rows, hot, arrays, ctx, kvs, group, side, factor)

    half = head_dim // 2
    frequency = jnp.exp(
        jnp.arange(half, dtype=F32) * (-2.0 * math.log(500000.0) / head_dim)
    )
    offset = prefix_keys.shape[0] * shards + (2 * c + p) * new_dev
    positions = offset + jnp.arange(new_dev, dtype=jnp.int32)
    angles = positions.astype(F32)[:, None] * frequency[None, :]
    cosine, sine = jnp.cos(angles), jnp.sin(angles)
    fresh_kv = finish_new(
        jnp.concatenate([cosine, cosine], 1), jnp.concatenate([-sine, sine], 1), own, got
    )
    other_kv = send(fresh_kv, "pool", 1, 2)
    parts = fresh(pos, q_rows, fresh_kv, other_kv, o, lse, ctx, kvs, group, factor)
    rows = o.shape[2]
    parts = [parts[0]] + [send(x, "ctx", s + 1, ctx) for s, x in enumerate(parts[1:])]
    mine = merge(parts, kvs, group, rows)
    pieces = [mine] + [send(mine, "ctx", s, ctx) for s in range(1, ctx)]
    others = [send(x, "pool", 1, 2) for x in pieces]
    halves = []
    for item in (pieces, others):
        result = out_project(pos, out_weight, item, ctx, peers)
        total = result[0]
        for r in range(1, peers):
            total = total + send(result[r], "head", r, peers).astype(F32)
        halves.append(total.astype(BF16))
    chunk = rows // group
    count = ctx // peers
    halves = [x.reshape(count, 1, chunk, -1) for x in halves]
    first = jnp.where(p == 0, halves[0], halves[1])
    second = jnp.where(p == 0, halves[1], halves[0])
    projected = jnp.concatenate([first, second], 1).reshape(2 * count * chunk, -1)
    new_keys = fresh_kv[:, :width].reshape(new_dev, kvs, head_dim)
    new_values = fresh_kv[:, width:].reshape(new_dev, kvs, head_dim)
    return projected, new_keys, new_values


def solution(mesh):
    in_specs = (
        P(None, "head", None),
        P(("ctx", "pool"), "head", None),
        P(("ctx", "pool"), "head", None),
        P(None, ("ctx", "pool")),
        P(("ctx", "pool"), "head"),
        P(("ctx", "pool"), "head"),
        P(("ctx", "pool"), None, "head", None),
        P(("ctx", "pool"), None, "head", None),
        P(("ctx", "pool")),
        P(),
        P("head", ("ctx", "pool")),
    )
    out_specs = (
        P("head", ("ctx", "pool")),
        P(("ctx", "pool"), "head", None),
        P(("ctx", "pool"), "head", None),
    )
    return jax.shard_map(body, mesh=mesh, in_specs=in_specs, out_specs=out_specs, check_vma=False)
```
